256 devices in a mesh: theta: 128 (over y_hi, x, z, core), gz: 2 (over y_lo).
Axes of the slice: x: 4, y: 4 (y_hi: 2, y_lo: 2; y = y_hi * 2 + y_lo), z: 8, core: 2. Of those that a mesh axis runs over, the one named last changes fastest.
Arguments:
- field: float32 [16, 8192, 1024], P('gz', 'theta'), parts along dimension 0, may hold values from -6 to 6
- courant: float32 [1024], replicated, may hold values from 0.2 to 0.8
Outputs:
- advanced: float32 [16, 8192, 1024], P('gz', 'theta'), parts along dimension 0
The draws below stay inside these ranges and needn't reach their ends.
There are 2 independent parts, one for each index of `gz`. The reference program is written for one: setup_inputs(seed, part) draws one part's arguments, and reference() takes and returns one part's arrays. A program takes and returns all parts, laid end to end along the dimension named above; an argument that names none is the same for every part. Nothing has to cross between parts.
All inputs are finite; a program needn't handle non-finite values.
Results may differ from the reference program's by a relative error of at most 0.00007.
Values sent between devices are 32-bit elements; how exact they have to be, the bound alone decides.
No kernel may reach another device: no remote copies, remote signals or barrier semaphores. Data moves between devices by JAX's collectives and lax.ppermute only.
A program may use at most 128 MiB of HBM per device.

```python
import math
import jax
import jax.numpy as jnp
from jax import lax

NR = 1024
H = 8
NTH = 8192


def shard_levels(key, dims, shards, least, high):
    gain, own = 1.0, jax.random.fold_in(key, 6)
    for axis_at, blocks in shards:
        steps = jnp.exp(jax.random.uniform(jax.random.fold_in(own, axis_at), (blocks,), jnp.float32, least / len(shards), high / len(shards)))
        gain = gain * jnp.repeat(steps, dims[axis_at] // blocks).reshape([-1 if axis == axis_at else 1 for axis in range(len(dims))])
    return gain


def noise(own_key, dims, deviation, most, split=(), kind=jnp.bfloat16):
    factor_of = shard_levels(own_key, dims, split, -0.22, 0.18) if split else 1.0
    entries = jax.random.normal(own_key, dims, jnp.float32) * deviation * factor_of
    return jnp.minimum(jnp.maximum(entries, -most), most).astype(kind)


def setup_inputs(seed: int = 0, part: int = 0) -> dict:
    streams_of = jax.random.split(jax.random.key(seed), 3)
    own_keys = jax.random.split(jax.random.fold_in(streams_of[2], part), 3)
    return {
        "field": noise(own_keys[0], (H, NTH, NR), 1.0, 6.0, ((1, 128),), jnp.float32),
        "courant": jnp.clip(jnp.exp(jax.random.uniform(streams_of[1], (NR,), jnp.float32, math.log(0.2), math.log(0.8))), 0.2, 0.8),
    }


stencil_weights = (4.0 / 5.0, -1.0 / 5.0, 4.0 / 105.0, -1.0 / 280.0)
radial_step = 0.2


def diameter_blocks(radial_count):
    intervals = 2 * radial_count - 1
    row_index = jnp.arange(radial_count, dtype=jnp.int32)[:, None]
    col_index = jnp.arange(2 * radial_count, dtype=jnp.int32)[None, :]
    angle_unit = math.pi / (2 * intervals)
    summed = (row_index + col_index).astype(jnp.float32) * angle_unit
    differ = (row_index - col_index).astype(jnp.float32) * angle_unit
    spacing = -2.0 * jnp.sin(summed) * jnp.sin(differ)
    same = row_index == col_index
    row_factor = jnp.where(row_index == 0, 2.0, 1.0).astype(jnp.float32)
    col_factor = jnp.where((col_index == 0) | (col_index == intervals), 2.0, 1.0).astype(jnp.float32)
    parity = jnp.where((row_index + col_index) % 2 == 0, 1.0, -1.0).astype(jnp.float32)
    safe_spacing = jnp.where(same, 1.0, spacing)
    offdiag = jnp.where(same, 0.0, row_factor / col_factor * parity / safe_spacing)
    matrix = offdiag - jnp.where(same, jnp.sum(offdiag, axis=1, keepdims=True), 0.0)
    near = matrix[:, :radial_count].T
    far = matrix[:, radial_count:][:, ::-1].T
    return near, far


def radial_weight(radial_count):
    intervals = 2 * radial_count - 1
    angles = jnp.arange(radial_count, dtype=jnp.int32).astype(jnp.float32) * (math.pi / intervals)
    return jnp.sin(angles) ** 2


def azimuth_difference(extended, rows):
    total = jnp.zeros((extended.shape[0], rows, extended.shape[2]), jnp.float32)
    for offset in range(1, 5):
        total = total + stencil_weights[offset - 1] * (extended[:, 4 + offset:4 + offset + rows] - extended[:, 4 - offset:4 - offset + rows])
    return total


def reference(field, courant):
    near, far = diameter_blocks(NR)
    weight = radial_weight(NR)
    tau = radial_step / (2 * NR - 1)

    def section_rate(state):
        padded = jnp.concatenate([state[:, -4:], state, state[:, :4]], axis=1)
        azimuth = azimuth_difference(padded, NTH)
        opposite = jnp.roll(state, NTH // 2, axis=1)
        deriv = jnp.dot(state.reshape(-1, NR), near, precision=lax.Precision.HIGHEST) + jnp.dot(opposite.reshape(-1, NR), far, precision=lax.Precision.HIGHEST)
        deriv = deriv.reshape(state.shape)
        return -courant * azimuth - tau * weight * state * deriv

    first = field + section_rate(field)
    second = 0.75 * field + 0.25 * (first + section_rate(first))
    return field / 3.0 + (2.0 / 3.0) * (second + section_rate(second))
```

```python
import functools
import math

import jax
import jax.numpy as jnp
import ml_dtypes
import numpy as np
from jax import lax
from jax.experimental import pallas as pl
from jax.experimental.pallas import tpu as pltpu
from jax.sharding import PartitionSpec as P

stencil_weights = (4.0 / 5.0, -1.0 / 5.0, 4.0 / 105.0, -1.0 / 280.0)
radial_step = 0.2
rank = 24
lines = 8
halo = 12
f32 = jnp.float32
bf16 = jnp.bfloat16


def split_table(a):
    hi = a.astype(ml_dtypes.bfloat16)
    lo = (a - hi.astype(np.float64)).astype(ml_dtypes.bfloat16)
    return hi, lo


def cross_factors(block, terms):
    rest = block.copy()
    left, right = [], []
    for _ in range(terms):
        at = np.unravel_index(np.argmax(np.abs(rest)), rest.shape)
        column = rest[:, at[1]] / rest[at]
        row = rest[at[0], :].copy()
        left.append(column)
        right.append(row)
        rest = rest - column[:, None] * row[None, :]
    return np.stack(left, axis=1), np.stack(right, axis=0)


@functools.lru_cache(maxsize=None)
def tables(count):
    intervals = 2 * count - 1
    row = np.arange(count)[:, None]
    col = np.arange(2 * count)[None, :]
    sines = np.array([math.sin(math.pi * k / (2 * intervals)) for k in range(3 * count)])
    same = row == col
    spacing = -2.0 * sines[row + col] * np.sign(row - col) * sines[np.abs(row - col)]
    row_factor = np.where(row == 0, 2.0, 1.0)
    col_factor = np.where((col == 0) | (col == intervals), 2.0, 1.0)
    parity = np.where((row + col) % 2 == 0, 1.0, -1.0)
    off = np.where(same, 0.0, row_factor / col_factor * parity / np.where(same, 1.0, spacing))
    matrix = off - np.where(same, off.sum(axis=1, keepdims=True), 0.0)
    near = matrix[:, :count].T
    far = matrix[:, count:][:, ::-1].T
    scale = -(radial_step / intervals) * sines[2 * np.arange(count)] ** 2
    left, right = cross_factors(far, rank)
    near_hi, near_lo = split_table(near * scale[None, :])
    left_hi, left_lo = split_table(left)
    right_hi, right_lo = split_table(right * scale[None, :])
    left_both = np.zeros((count, 128), ml_dtypes.bfloat16)
    left_both[:, :rank] = left_hi
    left_both[:, rank : 2 * rank] = left_lo
    right_all = np.concatenate([right_hi, right_hi, right_lo, right_lo], axis=0)
    return near_hi, near_lo, left_both, right_all


def halves(x):
    hi = x.astype(bf16)
    lo = (x - hi.astype(f32)).astype(bf16)
    return hi, lo


def dot(a, b):
    return jnp.dot(a, b, preferred_element_type=f32)


def near_product(hi, lo, near_hi, near_lo):
    return dot(hi, near_hi) + dot(lo, near_hi) + dot(hi, near_lo)


def projected(hi, lo, left_both):
    both = (dot(hi, left_both) + dot(lo, left_both)).T
    return both[:rank] + both[rank : 2 * rank]


def edges_kernel(par, field, to_pair, to_other):
    first = [jnp.swapaxes(field[:, 0:16, :], 0, 1)[:halo].reshape(halo * lines, -1)]
    last = [jnp.swapaxes(field[:, 48:64, :], 0, 1)[16 - halo :].reshape(halo * lines, -1)]

    @pl.when(par[0] == 0)
    def _():
        to_pair[...] = last[0]
        to_other[...] = first[0]

    @pl.when(par[0] != 0)
    def _():
        to_pair[...] = first[0]
        to_other[...] = last[0]


def own_kernel(field, near_hi, near_lo, left_both, state, product, proj):
    for at in range(0, 64, 16):
        rows = jnp.swapaxes(field[:, at : at + 16, :], 0, 1).reshape(16 * lines, -1)
        span = slice(at * lines, (at + 16) * lines)
        state[span, :] = rows
        hi, lo = halves(rows)
        product[span, :] = near_product(hi, lo, near_hi[...], near_lo[...])
        proj[:, span] = projected(hi, lo, left_both[...])


def join_kernel(par, own, proj_own, from_pair, from_other, left_both, state, proj):
    wide = halo * lines
    total = own.shape[0]
    state[wide : wide + total, :] = own[...]

    @pl.when(par[0] == 0)
    def _():
        state[:wide, :] = from_other[...]
        state[wide + total :, :] = from_pair[...]

    @pl.when(par[0] != 0)
    def _():
        state[:wide, :] = from_pair[...]
        state[wide + total :, :] = from_other[...]

    rows = jnp.concatenate([state[32:wide, :], state[wide + total : wide + total + 64, :]], axis=0)
    hi, lo = halves(rows)
    proj[:, :total] = proj_own[...]
    proj[:, total:] = projected(hi, lo, left_both[...])


def azimuth(state, courant, start, count):
    window = state[start : start + count + 64, :]
    total = None
    for q in range(1, 5):
        upper = window[32 + 8 * q : 32 + 8 * q + count, :]
        lower = window[32 - 8 * q : 32 - 8 * q + count, :]
        term = stencil_weights[q - 1] * (upper - lower)
        total = term if total is None else total + term
    return window[32 : 32 + count, :] - courant * total


def first_rate_kernel(state, own_product, courant, near_hi, near_lo, partial, product):
    wide = halo * lines
    total = own_product.shape[0]
    speed = courant[...]
    for at in range(0, total + 128, 64):
        partial[at : at + 64, :] = azimuth(state, speed, at, 64)
    product[64 : 64 + total, :] = own_product[...]
    rows = jnp.concatenate([state[32:wide, :], state[wide + total : wide + total + 64, :]], axis=0)
    hi, lo = halves(rows)
    both = near_product(hi, lo, near_hi[...], near_lo[...])
    product[:64, :] = both[:64]
    product[64 + total :, :] = both[64:]


def rate_kernel(old, new, field_at, state, field, courant, near_hi, near_lo, partial, product):
    speed = courant[...]
    count = partial.shape[0]
    step = 64
    for at in range(0, count, step):
        ahead = azimuth(state, speed, at, step)
        partial[at : at + step, :] = old * field[field_at + at : field_at + at + step, :] + new * ahead
    chunk = count // 4 if count % 64 == 0 and count // 4 % 16 == 0 else 64
    for at in range(0, count, chunk):
        hi, lo = halves(state[32 + at : 32 + at + chunk, :])
        product[at : at + chunk, :] = new * near_product(hi, lo, near_hi[...], near_lo[...])


def opposite_stack(proj, new):
    value = proj if new is None else new * proj
    hi = value.astype(bf16).astype(f32)
    lo = value - hi
    return jnp.concatenate([hi, lo, hi, lo], axis=0).astype(bf16).T


def advance(at, step, stack_rows, state, partial, product, right_all):
    far = dot(stack_rows, right_all)
    return partial[at : at + step, :] + state[32 + at : 32 + at + step, :] * (
        product[at : at + step, :] + far
    )


def advance_kernel(new, offset, ordered, opposite, state, partial, product, right_all, left_both, ahead, proj):
    stack = opposite_stack(opposite[...], new)
    if not ordered:
        stack = jnp.concatenate([stack[-128:-64], stack[:-128], stack[-64:]], axis=0)
    step = 64
    count = ahead.shape[0]
    for at in range(0, count, step):
        rows = advance(at, step, stack[at : at + step], state, partial, product, right_all[...])
        ahead[at : at + step, :] = rows
    inner = proj.shape[1]
    hi, lo = halves(ahead[32 : 32 + inner, :])
    proj[...] = projected(hi, lo, left_both[...])


def last_kernel(new, opposite, state, partial, product, right_all, out):
    stack = opposite_stack(opposite[...], new)
    for at in range(0, 512, 64):
        rows = advance(at, 64, stack[at : at + 64], state, partial, product, right_all[...])
        out[:, at // 8 : at // 8 + 8, :] = jnp.swapaxes(rows.reshape(8, lines, -1), 0, 1)


def on_chip(count):
    return [pl.BlockSpec(memory_space=pltpu.VMEM)] * count


def run(kernel, outs, *args, scalars=0, name):
    single = not isinstance(outs[0], tuple)
    shapes = [outs] if single else outs
    specs = [pl.BlockSpec(memory_space=pltpu.SMEM)] * scalars + on_chip(len(args) - scalars)
    result = pl.pallas_call(
        kernel,
        out_shape=[jax.ShapeDtypeStruct(s, f32) for s in shapes],
        in_specs=specs,
        out_specs=on_chip(len(shapes)),
        compiler_params=pltpu.CompilerParams(vmem_limit_bytes=16 << 20),
        name=name,
    )(*args)
    return result[0] if single else result


def body(field, courant):
    count = field.shape[2]
    cells = field.shape[1] * lines
    size = lax.axis_size("theta")
    opposite = [(i, (i + size // 2) % size) for i in range(size)]
    pair = [(i, i ^ 1) for i in range(size)]
    other = [(i, (i + 1 if i % 2 else i - 1) % size) for i in range(size)]
    near_hi, near_lo, left_both, right_all = (jnp.asarray(t) for t in tables(count))
    par = (lax.axis_index("theta") % 2).astype(jnp.int32).reshape(1)
    speed = courant.reshape(1, count)
    edge = (halo * lines, count)

    to_pair, to_other = run(edges_kernel, [edge, edge], par, field, scalars=1, name="edges")
    from_pair = lax.ppermute(to_pair, "theta", pair)
    from_other = lax.ppermute(to_other, "theta", other)
    own, own_product, own_proj = run(
        own_kernel, [(cells, count), (cells, count), (rank, cells)],
        field, near_hi, near_lo, left_both, name="own",
    )
    start, proj = run(
        join_kernel, [(cells + 192, count), (rank, cells + 128)],
        par, own, own_proj, from_pair, from_other, left_both, scalars=1, name="join",
    )
    proj = lax.ppermute(proj, "theta", opposite)
    partial, product = run(
        first_rate_kernel, [(cells + 128, count), (cells + 128, count)],
        start, own_product, speed, near_hi, near_lo, name="rate1",
    )
    first, proj = run(
        functools.partial(advance_kernel, None, 32, False),
        [(cells + 128, count), (rank, cells + 64)],
        proj, start, partial, product, right_all, left_both, name="advance1",
    )
    proj = lax.ppermute(proj, "theta", opposite)
    partial, product = run(
        functools.partial(rate_kernel, 0.75, 0.25, 64), [(cells + 64, count), (cells + 64, count)],
        first, start, speed, near_hi, near_lo, name="rate2",
    )
    second, proj = run(
        functools.partial(advance_kernel, 0.25, 32, True), [(cells + 64, count), (rank, cells)],
        proj, first, partial, product, right_all, left_both, name="advance2",
    )
    proj = lax.ppermute(proj, "theta", opposite)
    partial, product = run(
        functools.partial(rate_kernel, 1.0 / 3.0, 2.0 / 3.0, 96), [(cells, count), (cells, count)],
        second, start, speed, near_hi, near_lo, name="rate3",
    )
    return run(
        functools.partial(last_kernel, 2.0 / 3.0), field.shape,
        proj, second, partial, product, right_all, name="advance3",
    )


def solution(mesh):
    placed = (P("gz", "theta", None), P())
    return jax.shard_map(
        body, mesh=mesh, in_specs=placed, out_specs=P("gz", "theta", None), check_vma=False
    )
```

```python
import functools
import math

import jax
import jax.numpy as jnp
import ml_dtypes
import numpy as np
from jax import lax
from jax.experimental import pallas as pl
from jax.experimental.pallas import tpu as pltpu
from jax.sharding import PartitionSpec as P

stencil_weights = (4.0 / 5.0, -1.0 / 5.0, 4.0 / 105.0, -1.0 / 280.0)
radial_step = 0.2
rank = 24
block_rank = 20
tile = 256
lines = 8
halo = 12
f32 = jnp.float32
bf16 = jnp.bfloat16


def split_table(a):
    hi = a.astype(ml_dtypes.bfloat16)
    lo = (a - hi.astype(np.float64)).astype(ml_dtypes.bfloat16)
    return hi, lo


def cross_factors(block, terms):
    rest = block.copy()
    left, right = [], []
    for _ in range(terms):
        at = np.unravel_index(np.argmax(np.abs(rest)), rest.shape)
        column = rest[:, at[1]] / rest[at]
        row = rest[at[0], :].copy()
        left.append(column)
        right.append(row)
        rest = rest - column[:, None] * row[None, :]
    return np.stack(left, axis=1), np.stack(right, axis=0)


@functools.lru_cache(maxsize=None)
def tables(count):
    intervals = 2 * count - 1
    row = np.arange(count)[:, None]
    col = np.arange(2 * count)[None, :]
    sines = np.array([math.sin(math.pi * k / (2 * intervals)) for k in range(3 * count)])
    same = row == col
    spacing = -2.0 * sines[row + col] * np.sign(row - col) * sines[np.abs(row - col)]
    row_factor = np.where(row == 0, 2.0, 1.0)
    col_factor = np.where((col == 0) | (col == intervals), 2.0, 1.0)
    parity = np.where((row + col) % 2 == 0, 1.0, -1.0)
    off = np.where(same, 0.0, row_factor / col_factor * parity / np.where(same, 1.0, spacing))
    matrix = off - np.where(same, off.sum(axis=1, keepdims=True), 0.0)
    near = matrix[:, :count].T
    far = matrix[:, count:][:, ::-1].T
    scale = -(radial_step / intervals) * sines[2 * np.arange(count)] ** 2
    half = count // 2
    left = np.zeros((count, 64))
    across = np.zeros((64, count))
    left[:, :rank], right = cross_factors(far, rank)
    other = slice(rank, rank + block_rank)
    sibling = slice(rank + block_rank, rank + 2 * block_rank)
    for span, columns in ((half, other), (tile, sibling)):
        for at in range(0, count, span):
            to = at + span if (at // span) % 2 == 0 else at - span
            block = near[at : at + span, to : to + span]
            left[at : at + span, columns], across[columns, to : to + span] = cross_factors(
                block, block_rank
            )
    diagonal = np.concatenate(
        [near[at : at + tile, at : at + tile] for at in range(0, count, tile)], axis=1
    )
    diagonal_hi, diagonal_lo = split_table(diagonal * scale[None, :])
    across_hi, across_lo = split_table(across * scale[None, :])
    near_all = np.concatenate([diagonal_hi, diagonal_hi, diagonal_lo] + 4 * [across_hi] + 2 * [across_lo])
    left_both = np.concatenate(split_table(left), axis=1)
    right_hi, right_lo = split_table(right * scale[None, :])
    right_all = np.concatenate([right_hi, right_hi, right_lo, right_lo])
    return near_all, left_both, right_all


def halves(x):
    hi = x.astype(bf16)
    lo = (x - hi.astype(f32)).astype(bf16)
    return hi, lo


def dot(a, b):
    return jnp.dot(a, b, preferred_element_type=f32)


def columns_of(at, width=tile):
    return slice(at * width, (at + 1) * width)


def projected(hi, lo, left):
    parts = []
    for t in range(hi.shape[1] // tile):
        rows = columns_of(t)
        parts.append(dot(hi[:, rows], left[rows, :]) + dot(lo[:, rows], left[rows, :]))
    return parts


def far_values(parts):
    both = functools.reduce(jnp.add, parts).T
    return both[:rank] + both[64 : 64 + rank]


def near_tile(t, hi, lo, parts, near):
    place = lax.broadcasted_iota(jnp.int32, parts[0].shape, 1) % 64
    halves_sum = parts[2] + parts[3] if t < 2 else parts[0] + parts[1]
    values = jnp.where(place < rank + block_rank, halves_sum, parts[t ^ 1])
    value_hi, value_lo = halves(values)
    cols = columns_of(t)
    left = jnp.concatenate([hi[:, cols], lo[:, cols], hi[:, cols], value_hi, value_lo, value_hi], axis=1)
    return dot(left, near[:, cols])


def azimuth(state, courant, start, cells, lane):
    cols = columns_of(lane, 128)
    count = cells * lines
    window = state[start : start + count + 64, cols]
    total = None
    for q in range(1, 5):
        upper = window[32 + 8 * q : 32 + 8 * q + count, :]
        lower = window[32 - 8 * q : 32 - 8 * q + count, :]
        term = stencil_weights[q - 1] * (upper - lower)
        total = term if total is None else total + term
    return window[32 : 32 + count, :] - courant[:, cols] * total


def fetch(pairs, sems):
    copies = [pltpu.make_async_copy(source, target, sems.at[i]) for i, (source, target) in enumerate(pairs)]
    for copy in copies:
        copy.start()
    return copies


def await_all(copies):
    for copy in copies:
        copy.wait()


def own_section(wedge, near, left, state, product, proj):
    for at in range(0, 64, 16):
        rows = jnp.swapaxes(wedge[:, at : at + 16, :], 0, 1).reshape(16 * lines, -1)
        state[at * lines : (at + 16) * lines, :] = rows
    hi, lo = halves(state[...])
    parts = projected(hi, lo, left)
    proj[...] = far_values(parts)
    for t in range(4):
        product[:, columns_of(t)] = near_tile(t, hi, lo, parts, near)


def ends_kernel(place, to_pair, to_other, left, proj_pair, proj_other, rows):
    @pl.when(place[0] == 0)
    def _():
        rows[:64, :] = to_pair[32:, :]
        rows[64:, :] = to_other[:64, :]

    @pl.when(place[0] != 0)
    def _():
        rows[:64, :] = to_pair[:64, :]
        rows[64:, :] = to_other[32:, :]

    hi, lo = halves(rows[...])
    values = far_values(projected(hi, lo, left))
    proj_pair[...] = values[:, :64]
    proj_other[...] = values[:, 64:]


def inside_kernel(state, courant, partial):
    for lane in range(8):
        for at in range(0, 448, 112):
            partial[at : at + 112, columns_of(lane, 128)] = azimuth(state, courant, at, 14, lane)


def launch_kernel(place, field, near, left, to_pair, to_other, *refs):
    outs, (wedge, *here, sems) = refs[:3], refs[3:]
    first, middle, last = slice(0, 16), slice(16, 48), slice(48, 64)
    edges = fetch([(field.at[:, span, :], wedge.at[:, span, :]) for span in (first, last)], sems)

    def others():
        return [(field.at[:, middle, :], wedge.at[:, middle, :])] + list(zip((near, left), here))

    @pl.when(place[1] != 0)
    def _():
        fetch(others(), sems.at[2:])

    await_all(edges)
    low = jnp.swapaxes(wedge[:, first, :], 0, 1)[:halo].reshape(halo * lines, -1)
    high = jnp.swapaxes(wedge[:, last, :], 0, 1)[16 - halo :].reshape(halo * lines, -1)

    @pl.when(place[0] == 0)
    def _():
        to_pair[...] = high
        to_other[...] = low

    @pl.when(place[0] != 0)
    def _():
        to_pair[...] = low
        to_other[...] = high

    @pl.when(place[1] != 0)
    def _():
        await_all([pltpu.make_async_copy(*ends, sems.at[2 + i]) for i, ends in enumerate(others())])
        own_section(wedge, *here, *outs)


def own_kernel(place, field, near, left, *refs):
    done, outs, (wedge, *here, sems) = refs[:3], refs[3:6], refs[6:]

    @pl.when(place[1] == 0)
    def _():
        await_all(fetch([(field, wedge)] + list(zip((near, left), here)), sems))
        own_section(wedge, *here, *outs)

    @pl.when(place[1] != 0)
    def _():
        for out, ready in zip(outs, done):
            out[...] = ready[...]


def join_kernel(place, from_pair, from_other, own, courant, near, left, sides, partial, product):
    wide = halo * lines
    sides[0, wide:, :] = own[:64, :]
    sides[1, :64, :] = own[448:, :]

    @pl.when(place[0] == 0)
    def _():
        sides[0, :wide, :] = from_other[...]
        sides[1, 64:, :] = from_pair[...]

    @pl.when(place[0] != 0)
    def _():
        sides[0, :wide, :] = from_pair[...]
        sides[1, 64:, :] = from_other[...]

    rows = jnp.concatenate([sides[0, 32:wide, :], sides[1, 64:128, :]], axis=0)
    hi, lo = halves(rows)
    parts = projected(hi, lo, left)
    for t in range(4):
        both = near_tile(t, hi, lo, parts, near)
        product[0, :, columns_of(t)] = both[:64]
        product[1, :, columns_of(t)] = both[64:]
    for lane in range(8):
        for side in range(2):
            partial[side, :, columns_of(lane, 128)] = azimuth(sides.at[side], courant, 0, 12, lane)


def rate_kernel(old, new, cells, state, hi, lo, parts, own, sides, courant, near, partial, product):
    count = partial.shape[0]
    extra = (count - own.shape[0]) // 2
    pieces = [parts[:, columns_of(t, 128)] for t in range(4)]
    for t in range(4):
        product[:, columns_of(t)] = new * near_tile(t, hi, lo, pieces, near)
        for lane in (2 * t, 2 * t + 1):
            cols = columns_of(lane, 128)
            for at in range(0, count, cells * lines):
                end = at + cells * lines
                field = own[max(at - extra, 0) : min(end - extra, own.shape[0]), cols]
                if at < extra:
                    field = jnp.concatenate([sides[0, 96 - extra : 96, cols], field], axis=0)
                if end > count - extra:
                    field = jnp.concatenate([field, sides[1, 64 : 64 + extra, cols]], axis=0)
                ahead = azimuth(state, courant, at, cells, lane)
                partial[at:end, cols] = old * field + new * ahead


def opposite_stack(proj, new):
    value = new * proj
    hi = value.astype(bf16).astype(f32)
    lo = value - hi
    return jnp.concatenate([hi, lo, hi, lo], axis=0).astype(bf16).T


def advanced_rows(partial, state, product, stack_rows, right):
    return partial + state * (product + dot(stack_rows, right[...]))


def finish(ahead, left, hi_out, lo_out, parts_out, proj):
    inner = proj.shape[1]
    hi, lo = halves(ahead[32 : 32 + inner, :])
    hi_out[...] = hi
    lo_out[...] = lo
    parts = projected(hi, lo, left)
    for t in range(4):
        parts_out[:, columns_of(t, 128)] = parts[t]
    proj[...] = far_values(parts)


def first_kernel(place, opposite, by_other, by_pair, own, partial, product, sides, side_partial, side_product,
                 right, left, ahead, hi, lo, parts, proj, ends):
    near_pair = opposite_stack(by_pair[...], 1.0)
    near_other = opposite_stack(by_other[...], 1.0)

    @pl.when(place[0] == 0)
    def _():
        ends[0] = near_other
        ends[1] = near_pair

    @pl.when(place[0] != 0)
    def _():
        ends[0] = near_pair
        ends[1] = near_other

    stack = opposite_stack(opposite[...], 1.0)
    ahead[:64, :] = advanced_rows(side_partial[0, :64], sides[0, 32:96], side_product[0], ends[0], right)
    ahead[576:, :] = advanced_rows(side_partial[1, 32:], sides[1, 64:128], side_product[1], ends[1], right)
    low = side_partial[0, 64:]
    high = side_partial[1, :32]
    for at in range(0, 512, 128):
        inside = partial[max(at - 32, 0) : min(at + 96, 448)]
        if at == 0:
            inside = jnp.concatenate([low, inside], axis=0)
        if at == 384:
            inside = jnp.concatenate([inside, high], axis=0)
        rows = slice(at, at + 128)
        ahead[64 + at : 192 + at, :] = advanced_rows(inside, own[rows], product[rows], stack[rows], right)
    finish(ahead, left, hi, lo, parts, proj)


def second_kernel(new, opposite, state, partial, product, right, left, ahead, hi, lo, parts, proj):
    stack = opposite_stack(opposite[...], new)
    step = 144
    for at in range(0, ahead.shape[0], step):
        rows = slice(at, at + step)
        ahead[rows, :] = advanced_rows(
            partial[rows], state[32 + at : 32 + at + step], product[rows], stack[rows], right
        )
    finish(ahead, left, hi, lo, parts, proj)


def last_kernel(new, opposite, state, partial, product, right, out):
    stack = opposite_stack(opposite[...], new)
    for at in range(0, 512, 64):
        rows = slice(at, at + 64)
        done = advanced_rows(partial[rows], state[32 + at : 96 + at], product[rows], stack[rows], right)
        out[:, at // 8 : at // 8 + 8, :] = jnp.swapaxes(done.reshape(8, lines, -1), 0, 1)


def shape_of(*dims, dtype=f32):
    return jax.ShapeDtypeStruct(dims, dtype)


def run(kernel, outs, *args, name, flops, scalars=0, away=(), scratch=()):
    spaces = [pltpu.SMEM if i < scalars else pltpu.HBM if i in away else pltpu.VMEM for i in range(len(args))]
    return pl.pallas_call(
        kernel,
        out_shape=outs,
        in_specs=[pl.BlockSpec(memory_space=space) for space in spaces],
        out_specs=jax.tree.map(lambda _: pl.BlockSpec(memory_space=pltpu.VMEM), outs),
        scratch_shapes=scratch,
        compiler_params=pltpu.CompilerParams(vmem_limit_bytes=16 << 20),
        cost_estimate=pl.CostEstimate(flops=flops, transcendentals=0, bytes_accessed=0),
        name=name,
    )(*args)


def body(field, courant):
    count = field.shape[2]
    cells = field.shape[1] * lines
    size = lax.axis_size("theta")
    half = size // 2
    opposite = [(i, (i + half) % size) for i in range(size)]
    pair = [(i, i ^ 1) for i in range(size)]
    other = [(i, (i + 1 if i % 2 else i - 1) % size) for i in range(size)]
    far_pair = [(i, (i + half + (-1 if i % 2 else 1)) % size) for i in range(size)]
    far_other = [(i, (i + half + (1 if i % 2 else -1)) % size) for i in range(size)]
    near, left, right = (jnp.asarray(t) for t in tables(count))
    index = lax.axis_index("theta").astype(jnp.int32)
    place = jnp.stack([index & 1, jnp.where((index & 14) == 14, 0, 1)])
    speed = courant.reshape(1, count)
    edge = shape_of(halo * lines, count)

    own_shapes = [shape_of(cells, count), shape_of(cells, count), shape_of(rank, cells)]
    at_rest = [pltpu.with_memory_space_constraint(a, pltpu.HBM) for a in (field, near, left)]
    room = [pltpu.VMEM(a.shape, a.dtype) for a in at_rest]
    to_pair, to_other, *early = run(
        launch_kernel, [edge, edge] + own_shapes, place, *at_rest, scalars=1, away=(1, 2, 3), name="launch",
        flops=1 << 30, scratch=room + [pltpu.SemaphoreType.DMA((5,))],
    )
    from_pair = lax.ppermute(to_pair, "theta", pair)
    from_other = lax.ppermute(to_other, "theta", other)
    proj_pair, proj_other = run(
        ends_kernel, [shape_of(rank, 64)] * 2, place, to_pair, to_other, left,
        scalars=1, name="ends", flops=0, scratch=[pltpu.VMEM((128, count), f32)],
    )
    by_other = lax.ppermute(proj_other, "theta", far_other)
    by_pair = lax.ppermute(proj_pair, "theta", far_pair)
    own, product, proj = run(
        own_kernel, own_shapes, place, *at_rest, *early, scalars=1, away=(1, 2, 3), name="own",
        flops=4 << 30, scratch=room + [pltpu.SemaphoreType.DMA((3,))],
    )
    proj = lax.ppermute(proj, "theta", opposite)
    partial = run(inside_kernel, shape_of(cells - 64, count), own, speed, name="inside", flops=0)
    sides, side_partial, side_product = run(
        join_kernel, [shape_of(2, 160, count), shape_of(2, 96, count), shape_of(2, 64, count)],
        place, from_pair, from_other, own, speed, near, left, scalars=1, name="join", flops=1 << 30,
    )

    def advanced_shapes(rows):
        inner = rows - 64
        return [shape_of(rows, count), shape_of(inner, count, dtype=bf16), shape_of(inner, count, dtype=bf16),
                shape_of(inner, 512), shape_of(rank, inner)]

    first, hi, lo, parts, proj = run(
        first_kernel, advanced_shapes(cells + 128),
        place, proj, by_other, by_pair, own, partial, product, sides, side_partial, side_product, right, left,
        scalars=1, scratch=[pltpu.VMEM((2, 64, 4 * rank), bf16)], name="advance1", flops=1 << 30,
    )
    proj = lax.ppermute(proj, "theta", opposite)
    partial, product = run(
        functools.partial(rate_kernel, 0.75, 0.25, 12), [shape_of(cells + 64, count)] * 2,
        first, hi, lo, parts, own, sides, speed, near, name="rate2", flops=3 << 30,
    )
    second, hi, lo, parts, proj = run(
        functools.partial(second_kernel, 0.25), advanced_shapes(cells + 64),
        proj, first, partial, product, right, left, name="advance2", flops=1 << 30,
    )
    proj = lax.ppermute(proj, "theta", opposite)
    partial, product = run(
        functools.partial(rate_kernel, 1.0 / 3.0, 2.0 / 3.0, 16), [shape_of(cells, count)] * 2,
        second, hi, lo, parts, own, sides, speed, near, name="rate3", flops=3 << 30,
    )
    return run(
        functools.partial(last_kernel, 2.0 / 3.0), shape_of(*field.shape),
        proj, second, partial, product, right, name="advance3", flops=1 << 30,
    )


def solution(mesh):
    placed = (P("gz", "theta", None), P())
    return jax.shard_map(
        body, mesh=mesh, in_specs=placed, out_specs=P("gz", "theta", None), check_vma=False
    )
```

```python
import functools
import math

import jax
import jax.numpy as jnp
import ml_dtypes
import numpy as np
from jax import lax
from jax.experimental import pallas as pl
from jax.experimental.pallas import tpu as pltpu
from jax.sharding import PartitionSpec as P

stencil_weights = (4.0 / 5.0, -1.0 / 5.0, 4.0 / 105.0, -1.0 / 280.0)
radial_step = 0.2
rank = 24
block_rank = 20
tile = 256
lines = 8
halo = 12
f32 = jnp.float32
bf16 = jnp.bfloat16


def split_table(a):
    hi = a.astype(ml_dtypes.bfloat16)
    lo = (a - hi.astype(np.float64)).astype(ml_dtypes.bfloat16)
    return hi, lo


def cross_factors(block, terms):
    rest = block.copy()
    left, right = [], []
    for _ in range(terms):
        at = np.unravel_index(np.argmax(np.abs(rest)), rest.shape)
        column = rest[:, at[1]] / rest[at]
        row = rest[at[0], :].copy()
        left.append(column)
        right.append(row)
        rest = rest - column[:, None] * row[None, :]
    return np.stack(left, axis=1), np.stack(right, axis=0)


@functools.lru_cache(maxsize=None)
def tables(count):
    intervals = 2 * count - 1
    row = np.arange(count)[:, None]
    col = np.arange(2 * count)[None, :]
    sines = np.array([math.sin(math.pi * k / (2 * intervals)) for k in range(3 * count)])
    same = row == col
    spacing = -2.0 * sines[row + col] * np.sign(row - col) * sines[np.abs(row - col)]
    row_factor = np.where(row == 0, 2.0, 1.0)
    col_factor = np.where((col == 0) | (col == intervals), 2.0, 1.0)
    parity = np.where((row + col) % 2 == 0, 1.0, -1.0)
    off = np.where(same, 0.0, row_factor / col_factor * parity / np.where(same, 1.0, spacing))
    matrix = off - np.where(same, off.sum(axis=1, keepdims=True), 0.0)
    near = matrix[:, :count].T
    far = matrix[:, count:][:, ::-1].T
    scale = -(radial_step / intervals) * sines[2 * np.arange(count)] ** 2
    half = count // 2
    left = np.zeros((count, 64))
    across = np.zeros((64, count))
    left[:, :rank], right = cross_factors(far, rank)
    other = slice(rank, rank + block_rank)
    sibling = slice(rank + block_rank, rank + 2 * block_rank)
    for span, columns in ((half, other), (tile, sibling)):
        for at in range(0, count, span):
            to = at + span if (at // span) % 2 == 0 else at - span
            block = near[at : at + span, to : to + span]
            left[at : at + span, columns], across[columns, to : to + span] = cross_factors(
                block, block_rank
            )
    diagonal = np.concatenate(
        [near[at : at + tile, at : at + tile] for at in range(0, count, tile)], axis=1
    )
    diagonal_hi, diagonal_lo = split_table(diagonal * scale[None, :])
    across_hi, across_lo = split_table(across * scale[None, :])
    near_all = np.concatenate([diagonal_hi, diagonal_hi, diagonal_lo] + 4 * [across_hi] + 2 * [across_lo])
    left_both = np.concatenate(split_table(left), axis=1)
    right_hi, right_lo = split_table(right * scale[None, :])
    right_all = np.concatenate([right_hi, right_hi, right_lo, right_lo])
    return near_all, left_both, right_all


def halves(x):
    hi = x.astype(bf16)
    lo = (x - hi.astype(f32)).astype(bf16)
    return hi, lo


def dot(a, b):
    return jnp.dot(a, b, preferred_element_type=f32)


def columns_of(at, width=tile):
    return slice(at * width, (at + 1) * width)


def projected(hi, lo, left):
    parts = []
    for t in range(hi.shape[1] // tile):
        rows = columns_of(t)
        parts.append(dot(hi[:, rows], left[rows, :]) + dot(lo[:, rows], left[rows, :]))
    return parts


def far_values(parts):
    both = functools.reduce(jnp.add, parts).T
    return both[:rank] + both[64 : 64 + rank]


def near_tile(t, hi, lo, parts, near):
    place = lax.broadcasted_iota(jnp.int32, parts[0].shape, 1) % 64
    halves_sum = parts[2] + parts[3] if t < 2 else parts[0] + parts[1]
    values = jnp.where(place < rank + block_rank, halves_sum, parts[t ^ 1])
    value_hi, value_lo = halves(values)
    cols = columns_of(t)
    left = jnp.concatenate([hi[:, cols], lo[:, cols], hi[:, cols], value_hi, value_lo, value_hi], axis=1)
    return dot(left, near[:, cols])


def azimuth(state, courant, start, cells, lane):
    cols = columns_of(lane, 128)
    count = cells * lines
    window = state[start : start + count + 64, cols]
    total = None
    for q in range(1, 5):
        upper = window[32 + 8 * q : 32 + 8 * q + count, :]
        lower = window[32 - 8 * q : 32 - 8 * q + count, :]
        term = stencil_weights[q - 1] * (upper - lower)
        total = term if total is None else total + term
    return window[32 : 32 + count, :] - courant[:, cols] * total


def launch_kernel(place, field, to_pair, to_other):
    low = jnp.swapaxes(field[:, :16, :], 0, 1)[:halo].reshape(halo * lines, -1)
    high = jnp.swapaxes(field[:, 48:, :], 0, 1)[16 - halo :].reshape(halo * lines, -1)

    @pl.when(place[0] == 0)
    def _():
        to_pair[...] = high
        to_other[...] = low

    @pl.when(place[0] != 0)
    def _():
        to_pair[...] = low
        to_other[...] = high


def own_kernel(place, field, left, state, hi_out, lo_out, parts_out, proj, proj_pair, proj_other):
    done = []
    for t in range(4):
        cols = columns_of(t)
        rows = jnp.swapaxes(field[:, :, cols], 0, 1).reshape(state.shape[0], tile)
        done.append(write_state(t, rows, left, state, hi_out, lo_out, parts_out, 0))
    values = far_values(done)
    proj[...] = values
    low, high = values[:, :64], values[:, -64:]

    @pl.when(place[0] == 0)
    def _():
        proj_pair[...] = high
        proj_other[...] = low

    @pl.when(place[0] != 0)
    def _():
        proj_pair[...] = low
        proj_other[...] = high


def inside_kernel(state, hi, lo, parts, courant, near, partial, product):
    pieces = [parts[:, columns_of(t, 128)] for t in range(4)]
    for t in range(4):
        product[:, columns_of(t)] = near_tile(t, hi, lo, pieces, near)
        for lane in (2 * t, 2 * t + 1):
            for at in range(0, 448, 112):
                partial[at : at + 112, columns_of(lane, 128)] = azimuth(state, courant, at, 14, lane)


def join_kernel(place, from_pair, from_other, own, courant, near, left, sides, partial, product):
    wide = halo * lines
    sides[0, wide:, :] = own[:64, :]
    sides[1, :64, :] = own[448:, :]

    @pl.when(place[0] == 0)
    def _():
        sides[0, :wide, :] = from_other[...]
        sides[1, 64:, :] = from_pair[...]

    @pl.when(place[0] != 0)
    def _():
        sides[0, :wide, :] = from_pair[...]
        sides[1, 64:, :] = from_other[...]

    rows = jnp.concatenate([sides[0, 32:wide, :], sides[1, 64:128, :]], axis=0)
    hi, lo = halves(rows)
    parts = projected(hi, lo, left)
    for t in range(4):
        both = near_tile(t, hi, lo, parts, near)
        product[0, :, columns_of(t)] = both[:64]
        product[1, :, columns_of(t)] = both[64:]
    for lane in range(8):
        for side in range(2):
            partial[side, :, columns_of(lane, 128)] = azimuth(sides.at[side], courant, 0, 12, lane)


def rate_kernel(old, new, cells, state, hi, lo, parts, own, sides, courant, near, partial, product):
    count = partial.shape[0]
    extra = (count - own.shape[0]) // 2
    pieces = [parts[:, columns_of(t, 128)] for t in range(4)]
    for t in range(4):
        product[:, columns_of(t)] = new * near_tile(t, hi, lo, pieces, near)
        for lane in (2 * t, 2 * t + 1):
            cols = columns_of(lane, 128)
            for at in range(0, count, cells * lines):
                end = at + cells * lines
                field = own[max(at - extra, 0) : min(end - extra, own.shape[0]), cols]
                if at < extra:
                    field = jnp.concatenate([sides[0, 96 - extra : 96, cols], field], axis=0)
                if end > count - extra:
                    field = jnp.concatenate([field, sides[1, 64 : 64 + extra, cols]], axis=0)
                ahead = azimuth(state, courant, at, cells, lane)
                partial[at:end, cols] = old * field + new * ahead


def opposite_stack(proj, new):
    value = new * proj
    hi = value.astype(bf16).astype(f32)
    lo = value - hi
    return jnp.concatenate([hi, lo, hi, lo], axis=0).astype(bf16).T


def write_state(t, rows, left, ahead, hi_out, lo_out, parts_out, skip=32):
    cols = columns_of(t)
    ahead[:, cols] = rows
    inner = parts_out.shape[0]
    hi, lo = halves(rows[skip : skip + inner])
    hi_out[:, cols] = hi
    lo_out[:, cols] = lo
    part = dot(hi, left[cols, :]) + dot(lo, left[cols, :])
    parts_out[:, columns_of(t, 128)] = part
    return part


def first_kernel(place, opposite, by_other, by_pair, own, partial, product, sides, side_partial, side_product,
                 right, left, ahead, hi, lo, parts, proj, stack):
    stack[64:576, :] = opposite_stack(opposite[...], 1.0)
    near_pair = opposite_stack(by_pair[...], 1.0)
    near_other = opposite_stack(by_other[...], 1.0)

    @pl.when(place[0] == 0)
    def _():
        stack[:64, :] = near_other
        stack[576:, :] = near_pair

    @pl.when(place[0] != 0)
    def _():
        stack[:64, :] = near_pair
        stack[576:, :] = near_other

    done = []
    for t in range(4):
        cols = columns_of(t)
        far = dot(stack[...], right[:, cols])
        low = side_partial[0, :64, cols] + sides[0, 32:96, cols] * (side_product[0, :, cols] + far[:64])
        high = side_partial[1, 32:, cols] + sides[1, 64:128, cols] * (side_product[1, :, cols] + far[576:])
        inside = jnp.concatenate(
            [side_partial[0, 64:, cols], partial[:, cols], side_partial[1, :32, cols]], axis=0
        )
        middle = inside + own[:, cols] * (product[:, cols] + far[64:576])
        rows = jnp.concatenate([low, middle, high], axis=0)
        done.append(write_state(t, rows, left, ahead, hi, lo, parts))
    proj[...] = far_values(done)


def second_kernel(new, opposite, state, partial, product, right, left, ahead, hi, lo, parts, proj):
    stack = opposite_stack(opposite[...], new)
    count = ahead.shape[0]
    done = []
    for t in range(4):
        cols = columns_of(t)
        far = dot(stack, right[:, cols])
        rows = partial[:, cols] + state[32 : 32 + count, cols] * (product[:, cols] + far)
        done.append(write_state(t, rows, left, ahead, hi, lo, parts))
    proj[...] = far_values(done)


def last_kernel(new, opposite, state, partial, product, right, out, done, sems):
    stack = opposite_stack(opposite[...], new)
    count = partial.shape[0]
    copies = []
    for t in range(4):
        cols = columns_of(t)
        far = dot(stack, right[:, cols])
        rows = partial[:, cols] + state[32 : 32 + count, cols] * (product[:, cols] + far)
        done[:, :, cols] = jnp.swapaxes(rows.reshape(count // lines, lines, tile), 0, 1)
        copies.append(pltpu.make_async_copy(done.at[:, :, cols], out.at[:, :, cols], sems.at[t]))
        copies[-1].start()
    for copy in copies:
        copy.wait()


def shape_of(*dims, dtype=f32):
    return jax.ShapeDtypeStruct(dims, dtype)


def run(kernel, outs, *args, name, flops, scalars=0, away=(), out_away=False, scratch=()):
    spaces = [pltpu.SMEM if i < scalars else pltpu.HBM if i in away else pltpu.VMEM for i in range(len(args))]
    return pl.pallas_call(
        kernel,
        out_shape=outs,
        in_specs=[pl.BlockSpec(memory_space=space) for space in spaces],
        out_specs=jax.tree.map(lambda _: pl.BlockSpec(memory_space=pltpu.HBM if out_away else pltpu.VMEM), outs),
        scratch_shapes=scratch,
        compiler_params=pltpu.CompilerParams(vmem_limit_bytes=16 << 20),
        cost_estimate=pl.CostEstimate(flops=flops, transcendentals=0, bytes_accessed=0),
        name=name,
    )(*args)


def body(field, courant):
    count = field.shape[2]
    cells = field.shape[1] * lines
    size = lax.axis_size("theta")
    half = size // 2
    opposite = [(i, (i + half) % size) for i in range(size)]
    pair = [(i, i ^ 1) for i in range(size)]
    other = [(i, (i + 1 if i % 2 else i - 1) % size) for i in range(size)]
    far_pair = [(i, (i + half + (-1 if i % 2 else 1)) % size) for i in range(size)]
    far_other = [(i, (i + half + (1 if i % 2 else -1)) % size) for i in range(size)]
    near, left, right = (jnp.asarray(t) for t in tables(count))
    index = lax.axis_index("theta").astype(jnp.int32)
    place = (index & 1).reshape(1)
    speed = courant.reshape(1, count)
    edge = shape_of(halo * lines, count)

    def state_shapes(rows, inner):
        return [shape_of(rows, count), shape_of(inner, count, dtype=bf16), shape_of(inner, count, dtype=bf16),
                shape_of(inner, 512), shape_of(rank, inner)]

    to_pair, to_other = run(launch_kernel, [edge, edge], place, field, scalars=1, name="launch", flops=0)
    from_pair = lax.ppermute(to_pair, "theta", pair)
    from_other = lax.ppermute(to_other, "theta", other)
    own, hi, lo, parts, proj, proj_pair, proj_other = run(
        own_kernel, state_shapes(cells, cells) + [shape_of(rank, 64)] * 2, place, field, left,
        scalars=1, name="own", flops=1 << 30,
    )
    by_other = lax.ppermute(proj_other, "theta", far_other)
    by_pair = lax.ppermute(proj_pair, "theta", far_pair)
    proj = lax.ppermute(proj, "theta", opposite)
    partial, product = run(
        inside_kernel, [shape_of(cells - 64, count), shape_of(cells, count)],
        own, hi, lo, parts, speed, near, name="inside", flops=4 << 30,
    )
    sides, side_partial, side_product = run(
        join_kernel, [shape_of(2, 160, count), shape_of(2, 96, count), shape_of(2, 64, count)],
        place, from_pair, from_other, own, speed, near, left, scalars=1, name="join", flops=1 << 30,
    )

    first, hi, lo, parts, proj = run(
        first_kernel, state_shapes(cells + 128, cells + 64),
        place, proj, by_other, by_pair, own, partial, product, sides, side_partial, side_product, right, left,
        scalars=1, scratch=[pltpu.VMEM((cells + 128, 4 * rank), bf16)], name="advance1", flops=1 << 30,
    )
    proj = lax.ppermute(proj, "theta", opposite)
    partial, product = run(
        functools.partial(rate_kernel, 0.75, 0.25, 12), [shape_of(cells + 64, count)] * 2,
        first, hi, lo, parts, own, sides, speed, near, name="rate2", flops=3 << 30,
    )
    second, hi, lo, parts, proj = run(
        functools.partial(second_kernel, 0.25), state_shapes(cells + 64, cells),
        proj, first, partial, product, right, left, name="advance2", flops=1 << 30,
    )
    proj = lax.ppermute(proj, "theta", opposite)
    partial, product = run(
        functools.partial(rate_kernel, 1.0 / 3.0, 2.0 / 3.0, 16), [shape_of(cells, count)] * 2,
        second, hi, lo, parts, own, sides, speed, near, name="rate3", flops=3 << 30,
    )
    return run(
        functools.partial(last_kernel, 2.0 / 3.0), shape_of(*field.shape),
        proj, second, partial, product, right, name="advance3", flops=1 << 30, out_away=True,
        scratch=[pltpu.VMEM(field.shape, f32), pltpu.SemaphoreType.DMA((4,))],
    )


def solution(mesh):
    placed = (P("gz", "theta", None), P())
    return jax.shard_map(
        body, mesh=mesh, in_specs=placed, out_specs=P("gz", "theta", None), check_vma=False
    )
```

```python
import functools
import math

import jax
import jax.numpy as jnp
import ml_dtypes
import numpy as np
from jax import lax
from jax.experimental import pallas as pl
from jax.experimental.pallas import tpu as pltpu
from jax.sharding import PartitionSpec as P

stencil_weights = (4.0 / 5.0, -1.0 / 5.0, 4.0 / 105.0, -1.0 / 280.0)
radial_step = 0.2
rank = 24
block_rank = 20
tile = 256
lines = 8
halo = 12
f32 = jnp.float32
bf16 = jnp.bfloat16


def split_table(a):
    hi = a.astype(ml_dtypes.bfloat16)
    lo = (a - hi.astype(np.float64)).astype(ml_dtypes.bfloat16)
    return hi, lo


def cross_factors(block, terms):
    rest = block.copy()
    left, right = [], []
    for _ in range(terms):
        at = np.unravel_index(np.argmax(np.abs(rest)), rest.shape)
        column = rest[:, at[1]] / rest[at]
        row = rest[at[0], :].copy()
        left.append(column)
        right.append(row)
        rest = rest - column[:, None] * row[None, :]
    return np.stack(left, axis=1), np.stack(right, axis=0)


@functools.lru_cache(maxsize=None)
def tables(count):
    intervals = 2 * count - 1
    row = np.arange(count)[:, None]
    col = np.arange(2 * count)[None, :]
    sines = np.array([math.sin(math.pi * k / (2 * intervals)) for k in range(3 * count)])
    same = row == col
    spacing = -2.0 * sines[row + col] * np.sign(row - col) * sines[np.abs(row - col)]
    row_factor = np.where(row == 0, 2.0, 1.0)
    col_factor = np.where((col == 0) | (col == intervals), 2.0, 1.0)
    parity = np.where((row + col) % 2 == 0, 1.0, -1.0)
    off = np.where(same, 0.0, row_factor / col_factor * parity / np.where(same, 1.0, spacing))
    matrix = off - np.where(same, off.sum(axis=1, keepdims=True), 0.0)
    near = matrix[:, :count].T
    far = matrix[:, count:][:, ::-1].T
    scale = -(radial_step / intervals) * sines[2 * np.arange(count)] ** 2
    half = count // 2
    left = np.zeros((count, 64))
    across = np.zeros((64, count))
    left[:, :rank], right = cross_factors(far, rank)
    other = slice(rank, rank + block_rank)
    sibling = slice(rank + block_rank, rank + 2 * block_rank)
    for span, columns in ((half, other), (tile, sibling)):
        for at in range(0, count, span):
            to = at + span if (at // span) % 2 == 0 else at - span
            block = near[at : at + span, to : to + span]
            left[at : at + span, columns], across[columns, to : to + span] = cross_factors(
                block, block_rank
            )
    diagonal = np.concatenate(
        [near[at : at + tile, at : at + tile] for at in range(0, count, tile)], axis=1
    )
    diagonal_hi, diagonal_lo = split_table(diagonal * scale[None, :])
    across_hi, across_lo = split_table(across * scale[None, :])
    near_all = np.concatenate([diagonal_hi, diagonal_hi, diagonal_lo] + 4 * [across_hi] + 2 * [across_lo])
    left_both = np.concatenate(split_table(left), axis=1)
    right_hi, right_lo = split_table(right * scale[None, :])
    right_all = np.concatenate([right_hi, right_hi, right_lo, right_lo])
    return near_all, left_both, right_all


def halves(x):
    hi = x.astype(bf16)
    lo = (x - hi.astype(f32)).astype(bf16)
    return hi, lo


def dot(a, b):
    return jnp.dot(a, b, preferred_element_type=f32)


def columns_of(at, width=tile):
    return slice(at * width, (at + 1) * width)


def projected(hi, lo, left):
    parts = []
    for t in range(hi.shape[1] // tile):
        rows = columns_of(t)
        parts.append(dot(hi[:, rows], left[rows, :]) + dot(lo[:, rows], left[rows, :]))
    return parts


def far_values(parts):
    both = functools.reduce(jnp.add, parts).T
    return both[:rank] + both[64 : 64 + rank]


def near_tile(t, rows, parts, near):
    place = lax.broadcasted_iota(jnp.int32, parts[0].shape, 1) % 64
    halves_sum = parts[2] + parts[3] if t < 2 else parts[0] + parts[1]
    values = jnp.where(place < rank + block_rank, halves_sum, parts[t ^ 1])
    value_hi, value_lo = halves(values)
    hi, lo = halves(rows)
    left = jnp.concatenate([hi, lo, hi, value_hi, value_lo, value_hi], axis=1)
    return dot(left, near[:, columns_of(t)])


def azimuth(state, courant, start, cells, lane):
    cols = columns_of(lane, 128)
    count = cells * lines
    window = state[start : start + count + 64, cols]
    total = None
    for q in range(1, 5):
        upper = window[32 + 8 * q : 32 + 8 * q + count, :]
        lower = window[32 - 8 * q : 32 - 8 * q + count, :]
        term = stencil_weights[q - 1] * (upper - lower)
        total = term if total is None else total + term
    return window[32 : 32 + count, :] - courant[:, cols] * total


def even():
    return lax.rem(lax.axis_index("theta"), 2) == 0


def launch_kernel(field, to_pair, to_other, wedge, sems):
    spans = (slice(0, 16), slice(48, 64), slice(16, 48))
    copies = [
        pltpu.make_async_copy(field.at[:, span, :], wedge.at[:, span, :], sems.at[i]) for i, span in enumerate(spans)
    ]
    for copy in copies:
        copy.start()
    for copy in copies[:2]:
        copy.wait()
    low = jnp.swapaxes(wedge[:, :16, :], 0, 1)[:halo].reshape(halo * lines, -1)
    high = jnp.swapaxes(wedge[:, 48:, :], 0, 1)[16 - halo :].reshape(halo * lines, -1)

    @pl.when(even())
    def _():
        to_pair[...] = high
        to_other[...] = low

    @pl.when(jnp.logical_not(even()))
    def _():
        to_pair[...] = low
        to_other[...] = high

    copies[2].wait()


def own_kernel(field, left, state, parts_out, proj, proj_pair, proj_other):
    done = []
    for t in range(4):
        cols = columns_of(t)
        rows = jnp.swapaxes(field[:, :, cols], 0, 1).reshape(state.shape[0], tile)
        done.append(write_state(t, rows, left, state, parts_out, 0))
    values = far_values(done)
    proj[...] = values
    low, high = values[:, :64], values[:, -64:]

    @pl.when(even())
    def _():
        proj_pair[...] = high
        proj_other[...] = low

    @pl.when(jnp.logical_not(even()))
    def _():
        proj_pair[...] = low
        proj_other[...] = high


def inside_kernel(state, parts, courant, near, partial, product):
    pieces = [parts[:, columns_of(t, 128)] for t in range(4)]
    for t in range(4):
        product[:, columns_of(t)] = near_tile(t, state[:, columns_of(t)], pieces, near)
        for lane in (2 * t, 2 * t + 1):
            for at in range(0, 448, 112):
                partial[at : at + 112, columns_of(lane, 128)] = azimuth(state, courant, at, 14, lane)


def join_kernel(from_pair, from_other, own, courant, near, left, sides, partial, product):
    wide = halo * lines
    sides[0, wide:, :] = own[:64, :]
    sides[1, :64, :] = own[448:, :]

    @pl.when(even())
    def _():
        sides[0, :wide, :] = from_other[...]
        sides[1, 64:, :] = from_pair[...]

    @pl.when(jnp.logical_not(even()))
    def _():
        sides[0, :wide, :] = from_pair[...]
        sides[1, 64:, :] = from_other[...]

    rows = jnp.concatenate([sides[0, 32:wide, :], sides[1, 64:128, :]], axis=0)
    hi, lo = halves(rows)
    parts = projected(hi, lo, left)
    for t in range(4):
        both = near_tile(t, rows[:, columns_of(t)], parts, near)
        product[0, :, columns_of(t)] = both[:64]
        product[1, :, columns_of(t)] = both[64:]
    for lane in range(8):
        for side in range(2):
            partial[side, :, columns_of(lane, 128)] = azimuth(sides.at[side], courant, 0, 12, lane)


def rate_kernel(old, new, cells, state, parts, own, sides, courant, near, partial, product):
    count = partial.shape[0]
    extra = (count - own.shape[0]) // 2
    pieces = [parts[:, columns_of(t, 128)] for t in range(4)]
    for t in range(4):
        product[:, columns_of(t)] = new * near_tile(t, state[32 : 32 + count, columns_of(t)], pieces, near)
        for lane in (2 * t, 2 * t + 1):
            cols = columns_of(lane, 128)
            for at in range(0, count, cells * lines):
                end = at + cells * lines
                field = own[max(at - extra, 0) : min(end - extra, own.shape[0]), cols]
                if at < extra:
                    field = jnp.concatenate([sides[0, 96 - extra : 96, cols], field], axis=0)
                if end > count - extra:
                    field = jnp.concatenate([field, sides[1, 64 : 64 + extra, cols]], axis=0)
                ahead = azimuth(state, courant, at, cells, lane)
                partial[at:end, cols] = old * field + new * ahead


def opposite_stack(proj, new):
    value = new * proj
    hi = value.astype(bf16).astype(f32)
    lo = value - hi
    return jnp.concatenate([hi, lo, hi, lo], axis=0).astype(bf16).T


def write_state(t, rows, left, ahead, parts_out, skip=32):
    cols = columns_of(t)
    ahead[:, cols] = rows
    inner = parts_out.shape[0]
    hi, lo = halves(rows[skip : skip + inner])
    part = dot(hi, left[cols, :]) + dot(lo, left[cols, :])
    parts_out[:, columns_of(t, 128)] = part
    return part


def first_kernel(opposite, by_other, by_pair, own, partial, product, sides, side_partial, side_product,
                 right, left, ahead, parts, proj, stack):
    stack[64:576, :] = opposite_stack(opposite[...], 1.0)
    near_pair = opposite_stack(by_pair[...], 1.0)
    near_other = opposite_stack(by_other[...], 1.0)

    @pl.when(even())
    def _():
        stack[:64, :] = near_other
        stack[576:, :] = near_pair

    @pl.when(jnp.logical_not(even()))
    def _():
        stack[:64, :] = near_pair
        stack[576:, :] = near_other

    done = []
    for t in range(4):
        cols = columns_of(t)
        far = dot(stack[...], right[:, cols])
        low = side_partial[0, :64, cols] + sides[0, 32:96, cols] * (side_product[0, :, cols] + far[:64])
        high = side_partial[1, 32:, cols] + sides[1, 64:128, cols] * (side_product[1, :, cols] + far[576:])
        inside = jnp.concatenate(
            [side_partial[0, 64:, cols], partial[:, cols], side_partial[1, :32, cols]], axis=0
        )
        middle = inside + own[:, cols] * (product[:, cols] + far[64:576])
        rows = jnp.concatenate([low, middle, high], axis=0)
        done.append(write_state(t, rows, left, ahead, parts))
    proj[...] = far_values(done)


def second_kernel(new, opposite, state, partial, product, right, left, ahead, parts, proj):
    stack = opposite_stack(opposite[...], new)
    count = ahead.shape[0]
    done = []
    for t in range(4):
        cols = columns_of(t)
        far = dot(stack, right[:, cols])
        rows = partial[:, cols] + state[32 : 32 + count, cols] * (product[:, cols] + far)
        done.append(write_state(t, rows, left, ahead, parts))
    proj[...] = far_values(done)


def last_kernel(new, opposite, state, partial, product, right, out, done, sems):
    stack = opposite_stack(opposite[...], new)
    count = partial.shape[0]
    copies = []
    for start, width in ((0, 256), (256, 256), (512, 256), (768, 128), (896, 128)):
        cols = slice(start, start + width)
        far = dot(stack, right[:, cols])
        rows = partial[:, cols] + state[32 : 32 + count, cols] * (product[:, cols] + far)
        done[:, :, cols] = jnp.swapaxes(rows.reshape(count // lines, lines, width), 0, 1)
        copies.append(pltpu.make_async_copy(done.at[:, :, cols], out.at[:, :, cols], sems.at[len(copies)]))
        copies[-1].start()
    for copy in copies:
        copy.wait()


def shape_of(*dims, dtype=f32):
    return jax.ShapeDtypeStruct(dims, dtype)


def run(kernel, outs, *args, name, flops, away=(), out_away=False, scratch=()):
    spaces = [pltpu.HBM if i in away else pltpu.VMEM for i in range(len(args))]
    return pl.pallas_call(
        kernel,
        out_shape=outs,
        in_specs=[pl.BlockSpec(memory_space=space) for space in spaces],
        out_specs=jax.tree.map(lambda _: pl.BlockSpec(memory_space=pltpu.HBM if out_away else pltpu.VMEM), outs),
        scratch_shapes=scratch,
        compiler_params=pltpu.CompilerParams(vmem_limit_bytes=16 << 20),
        cost_estimate=pl.CostEstimate(flops=flops, transcendentals=0, bytes_accessed=0),
        name=name,
    )(*args)


def body(field, courant):
    count = field.shape[2]
    cells = field.shape[1] * lines
    size = lax.axis_size("theta")
    half = size // 2
    opposite = [(i, (i + half) % size) for i in range(size)]
    pair = [(i, i ^ 1) for i in range(size)]
    other = [(i, (i + 1 if i % 2 else i - 1) % size) for i in range(size)]
    far_pair = [(i, (i + half + (-1 if i % 2 else 1)) % size) for i in range(size)]
    far_other = [(i, (i + half + (1 if i % 2 else -1)) % size) for i in range(size)]
    near, left, right = (jnp.asarray(t) for t in tables(count))
    speed = courant.reshape(1, count)
    edge = shape_of(halo * lines, count)

    def state_shapes(rows, inner):
        return [shape_of(rows, count), shape_of(inner, 512), shape_of(rank, inner)]

    to_pair, to_other, wedge = run(
        launch_kernel, [edge, edge, shape_of(*field.shape)], pltpu.with_memory_space_constraint(field, pltpu.HBM),
        away=(0,), name="launch", flops=0, scratch=[pltpu.SemaphoreType.DMA((3,))],
    )
    from_pair = lax.ppermute(to_pair, "theta", pair)
    from_other = lax.ppermute(to_other, "theta", other)
    own, parts, proj, proj_pair, proj_other = run(
        own_kernel, state_shapes(cells, cells) + [shape_of(rank, 64)] * 2, wedge, left,
        name="own", flops=1 << 30,
    )
    by_other = lax.ppermute(proj_other, "theta", far_other)
    by_pair = lax.ppermute(proj_pair, "theta", far_pair)
    proj = lax.ppermute(proj, "theta", opposite)
    partial, product = run(
        inside_kernel, [shape_of(cells - 64, count), shape_of(cells, count)],
        own, parts, speed, near, name="inside", flops=4 << 30,
    )
    sides, side_partial, side_product = run(
        join_kernel, [shape_of(2, 160, count), shape_of(2, 96, count), shape_of(2, 64, count)],
        from_pair, from_other, own, speed, near, left, name="join", flops=1 << 30,
    )

    first, parts, proj = run(
        first_kernel, state_shapes(cells + 128, cells + 64),
        proj, by_other, by_pair, own, partial, product, sides, side_partial, side_product, right, left,
        scratch=[pltpu.VMEM((cells + 128, 4 * rank), bf16)], name="advance1", flops=1 << 30,
    )
    proj = lax.ppermute(proj, "theta", opposite)
    partial, product = run(
        functools.partial(rate_kernel, 0.75, 0.25, 12), [shape_of(cells + 64, count)] * 2,
        first, parts, own, sides, speed, near, name="rate2", flops=3 << 30,
    )
    second, parts, proj = run(
        functools.partial(second_kernel, 0.25), state_shapes(cells + 64, cells),
        proj, first, partial, product, right, left, name="advance2", flops=1 << 30,
    )
    proj = lax.ppermute(proj, "theta", opposite)
    partial, product = run(
        functools.partial(rate_kernel, 1.0 / 3.0, 2.0 / 3.0, 16), [shape_of(cells, count)] * 2,
        second, parts, own, sides, speed, near, name="rate3", flops=3 << 30,
    )
    return run(
        functools.partial(last_kernel, 2.0 / 3.0), shape_of(*field.shape),
        proj, second, partial, product, right, name="advance3", flops=1 << 30, out_away=True,
        scratch=[pltpu.VMEM(field.shape, f32), pltpu.SemaphoreType.DMA((5,))],
    )


def solution(mesh):
    placed = (P("gz", "theta", None), P())
    return jax.shard_map(
        body, mesh=mesh, in_specs=placed, out_specs=P("gz", "theta", None), check_vma=False
    )
```
